32 devices in a mesh: tm: 16 (over z, y, x), batch: 2 (over core).
Axes of the slice: x: 2, y: 2, z: 4, core: 2. Of those that a mesh axis runs over, the one named last changes fastest.
Arguments:
- inputs: bfloat16 [2, 2048, 512], P('batch', 'tm'), may hold values from -30 to 30
- rates: bfloat16 [2, 2048, 1024], P('batch', 'tm'), may hold values from 9.765625e-06 to 0.7
- target: bfloat16 [2, 2048, 512], P('batch', 'tm'), may hold values from -30 to 30
- in_proj: bfloat16 [512, 1024], replicated, may hold values from -1 to 1
- out_proj: bfloat16 [512, 1024], replicated, may hold values from -0.1875 to 0.1875
Outputs:
- outputs: bfloat16 [2, 2048, 512], P('batch', 'tm')
- grad_in: float32 [512, 1024], P('tm')
- grad_out: float32 [512, 1024], P('tm')
The draws below stay inside these ranges and needn't reach their ends.
All inputs are finite; a program needn't handle non-finite values.
Results may differ from the reference program's by a relative error of at most 0.0049.
Values sent between devices are 32-bit elements; how exact they have to be, the bound alone decides.
A program may use at most 64 MiB of HBM per device.

```python
import jax
import jax.numpy as jnp
from jax import lax

D = 512
N = 1024
L_DEV = 128
BATCH = 2
TIME = 2048


def feature_field(key, salt):
    base = jax.random.fold_in(key, salt)
    key_a, key_b = jax.random.split(base, 2)
    ramp = 3.0 ** (jnp.arange(D, dtype=jnp.float32) / D)
    spread = jnp.exp(jax.random.uniform(key_a, (D,), jnp.float32, jnp.log(0.5), jnp.log(2.0)))
    scales = ramp * spread
    noise = jax.random.truncated_normal(key_b, -4.0, 4.0, (BATCH, TIME, D), jnp.float32)
    return noise * scales


def draw_inputs(key, part):
    return feature_field(key, 11).astype(jnp.bfloat16)


def draw_target(key, part):
    return feature_field(key, 23).astype(jnp.bfloat16)


def draw_rates(key, part):
    base = jax.random.fold_in(key, 37)
    keys = jax.random.split(base, 6)
    fast_share = 0.5
    picks = jax.random.uniform(keys[0], (BATCH, 1, N), jnp.float32) < fast_share
    fast = jnp.exp(jax.random.uniform(keys[1], (BATCH, 1, N), jnp.float32, jnp.log(1.0 / 50.0), jnp.log(1.0 / 30.0)))
    slow = jnp.exp(jax.random.uniform(keys[2], (BATCH, 1, N), jnp.float32, jnp.log(0.05), jnp.log(0.5))) / TIME
    base_rate = jnp.where(picks, fast, slow)
    nblocks = TIME // L_DEV
    factors = jnp.exp(jax.random.uniform(keys[3], (BATCH, nblocks, 1, N), jnp.float32, jnp.log(0.5), jnp.log(2.0)))
    spread = base_rate[:, None] * factors * jnp.ones((1, 1, L_DEV, 1), jnp.float32)
    spread = spread.reshape(BATCH, TIME, N)
    positions = jax.random.randint(keys[4], (BATCH, 2), 0, TIME)
    hits = jnp.any(jnp.arange(TIME)[None, :, None] == positions[:, None, :], axis=2)
    losses = -jnp.log(jax.random.uniform(keys[5], (BATCH, 1, N), jnp.float32, 0.5, 0.8))
    spread = jnp.where(hits[:, :, None], losses, spread)
    return spread.astype(jnp.bfloat16)


def draw_in_proj(key, part):
    base = jax.random.fold_in(key, 53)
    key_a, key_b = jax.random.split(base, 2)
    values = jax.random.truncated_normal(key_a, -4.0, 4.0, (D, N), jnp.float32)
    columns = jnp.exp(jax.random.uniform(key_b, (1, N), jnp.float32, jnp.log(0.3), jnp.log(3.0)))
    return (values * columns / jnp.sqrt(float(D))).astype(jnp.bfloat16)


def gaussian(rng, shape, scale, reach, kind=jnp.bfloat16):
    array = jax.random.normal(rng, shape, jnp.float32) * scale
    return jnp.minimum(jnp.maximum(array, -reach), reach).astype(kind)


def setup_inputs(seed: int = 0) -> dict:
    key_of = jax.random.split(jax.random.key(seed), 6)
    inputs = draw_inputs(jax.random.fold_in(key_of[5], 71), 0)
    rates = draw_rates(jax.random.fold_in(key_of[5], 71), 0)
    target = draw_target(jax.random.fold_in(key_of[5], 71), 0)
    in_proj = draw_in_proj(jax.random.fold_in(key_of[5], 71), 0)
    out_proj = gaussian(key_of[4], (D, N), N ** -0.5, 0.1875)
    return {"inputs": inputs, "rates": rates, "target": target, "in_proj": in_proj, "out_proj": out_proj}


def combine(earlier, latter):
    return (earlier[0] * latter[0], latter[0] * earlier[1] + latter[1])

def chain(decays, drives, reverse):
    time_len, channels = decays.shape
    dec_blocks = decays.reshape(time_len // L_DEV, L_DEV, channels)
    drv_blocks = drives.reshape(time_len // L_DEV, L_DEV, channels)

    def advance(carried, element):
        decayed, partial_value = lax.associative_scan(combine, element, axis=0, reverse=reverse)
        filled = partial_value + decayed * carried
        if reverse:
            boundary = filled[0]
        else:
            boundary = filled[-1]
        return (boundary, filled)
    start = jnp.zeros((channels,), jnp.float32)
    _, result = lax.scan(advance, start, (dec_blocks, drv_blocks), reverse=reverse)
    return result.reshape(time_len, channels)

def one_sequence(seq_inputs, seq_rates, seq_target, in_proj, out_proj):
    rates32 = seq_rates.astype(jnp.float32)
    decays = jnp.exp(-rates32)
    gates = jnp.sqrt(-jnp.expm1(-2.0 * rates32))
    drives = gates * jnp.dot(seq_inputs, in_proj, preferred_element_type=jnp.float32)
    states = chain(decays, drives, False)
    state_b = states.astype(jnp.bfloat16)
    mixed = jnp.dot(state_b, out_proj.T, preferred_element_type=jnp.float32)
    outputs = (seq_inputs.astype(jnp.float32) + mixed).astype(jnp.bfloat16)
    errors = (outputs.astype(jnp.float32) - seq_target.astype(jnp.float32)).astype(jnp.bfloat16)
    backed = jnp.dot(errors, out_proj, preferred_element_type=jnp.float32)
    next_decays = jnp.concatenate([decays[1:], jnp.ones((1, decays.shape[1]), decays.dtype)], 0)
    adjoint = chain(next_decays, backed, True)
    drive_grad = (gates * adjoint).astype(jnp.bfloat16)
    raw_in = jnp.dot(seq_inputs.T, drive_grad, preferred_element_type=jnp.float32)
    raw_out = jnp.dot(errors.T, state_b, preferred_element_type=jnp.float32)
    return (outputs, raw_in, raw_out)

def reference(inputs, rates, target, in_proj, out_proj):

    def per_sequence(packed):
        return one_sequence(packed[0], packed[1], packed[2], in_proj, out_proj)
    outputs, raw_in, raw_out = lax.map(per_sequence, (inputs, rates, target))
    sum_in = lax.optimization_barrier(jnp.sum(raw_in, axis=0))
    sum_out = lax.optimization_barrier(jnp.sum(raw_out, axis=0))
    squares = jnp.sum(sum_in * sum_in) + jnp.sum(sum_out * sum_out)
    rms_value = jnp.sqrt(squares / (2.0 * D * N) + 1e-06)
    factor = jnp.minimum(1.0, 1.0 / rms_value)
    return (outputs, factor * sum_in, factor * sum_out)
```

```python
import functools

import jax
import jax.numpy as jnp
from jax import lax
from jax.experimental import pallas as pl
from jax.experimental.pallas import tpu as pltpu
from jax.sharding import PartitionSpec as P

MESH = pl.DeviceIdType.MESH
SUB = 8
LANE = 128


def gate_of(rates, decays):
    sq = rates * rates
    poly = 1.0 / 39916800.0
    for den in (362880.0, 5040.0, 120.0, 6.0):
        poly = poly * sq + 1.0 / den
    poly = poly * sq + 1.0
    return jnp.sqrt(2.0 * decays * rates * poly)


def kernel(
    nt, nb, inputs_ref, rates_ref, target_ref, in_ref, out_ref,
    outputs_ref, gin_ref, gout_ref,
    dec, gat, val, part, fprod, bprod, seg, xall, eall, sall, dall, sblk, dblk,
    f1, f2, b1, b2, q1, q2, raw, acc, *rest,
):
    nbits = nt.bit_length() - 1
    recvs = rest[:nbits]
    c1s, c1r, c2s, c2r, xs, xr, rss, rsr = rest[nbits:]
    gs = 1 << (nbits // 2)
    ng = nt // gs
    length, width = inputs_ref.shape
    chans = in_ref.shape[1]
    cols = chans // nb
    steps = length // SUB
    nch, rows, cw = acc.shape[1], acc.shape[-2], acc.shape[-1]
    lanes = chans // LANE
    f32, bf16 = jnp.float32, jnp.bfloat16

    me = lax.axis_index("tm")
    mb = lax.axis_index("batch")
    grp, mem = me // gs, me % gs
    bits = [(me // (1 << q)) % 2 for q in range(nbits)]

    in_group = [grp * gs + (mem + d) % gs for d in range(gs)]
    in_line = [((grp + d) % ng) * gs + mem for d in range(ng)]
    in_batch = [(mb + d) % nb for d in range(nb)]

    barrier = pltpu.get_barrier_semaphore()
    peers = (
        [(t, mb) for t in in_group[1:]] + [(t, mb) for t in in_line[1:]] + [(me, b) for b in in_batch[1:]]
    )
    for peer in peers:
        pl.semaphore_signal(barrier, inc=1, device_id=peer, device_id_type=MESH)

    pending = []

    def send(src, dst, ssem, rsem, peer):
        cp = pltpu.make_async_remote_copy(
            src_ref=src, dst_ref=dst, send_sem=ssem, recv_sem=rsem, device_id=peer, device_id_type=MESH
        )
        cp.start()
        pending.append(cp)
        return cp

    def to_group(kind, buf):
        return [
            send(buf.at[0], buf.at[d], c1s.at[kind, d], c1r.at[kind, d], (in_group[d], mb)) for d in range(1, gs)
        ]

    def to_line(kind, buf):
        return [
            send(buf.at[0], buf.at[d], c2s.at[kind, d], c2r.at[kind, d], (in_line[d], mb)) for d in range(1, ng)
        ]

    def to_batch(kind, src_of, dst_of):
        return [
            send(src_of(d), dst_of(d), xs.at[kind, d], xr.at[kind, d], (me, in_batch[d])) for d in range(1, nb)
        ]

    def arrive(copies):
        for cp in copies:
            cp.wait_recv()

    def spread(ref, value):
        for l in range(lanes):
            ref[l] = value[:, l * LANE : (l + 1) * LANE]

    def take(ref, j):
        return jnp.concatenate([ref[l, pl.ds(j, SUB, stride=steps), :] for l in range(lanes)], axis=1)

    def put(ref, j, value):
        for l in range(lanes):
            ref[l // nch, l % nch, pl.ds(j, SUB, stride=steps), :] = value[:, l * LANE : (l + 1) * LANE]

    xall[0] = inputs_ref[...].astype(f32)
    rates = rates_ref[...].astype(f32)
    decays = jnp.exp(-rates)
    for l in range(lanes):
        dec[l, 0:length, :] = decays[:, l * LANE : (l + 1) * LANE]
        dec[l, length : length + SUB, :] = jnp.ones((SUB, LANE), f32)
    gates = gate_of(rates, decays)
    spread(gat, gates)
    spread(val, gates * jnp.dot(inputs_ref[...], in_ref[...], preferred_element_type=f32))

    row = lax.broadcasted_iota(jnp.int32, (SUB, chans), 0)

    run = jnp.zeros((SUB, chans), f32)
    prod = jnp.ones((SUB, chans), f32)
    for j in range(steps):
        d = take(dec, j)
        run = d * run + take(val, j)
        prod = d * prod
        part[j] = run
        fprod[j] = prod
    shift = 1
    while shift < SUB:
        keep = row >= shift
        run = jnp.where(keep, prod * pltpu.roll(run, shift, 0) + run, run)
        prod = jnp.where(keep, prod * pltpu.roll(prod, shift, 0), prod)
        shift *= 2
    seg[0] = jnp.where(row == 0, 1.0, pltpu.roll(prod, 1, 0))
    seg[1] = jnp.where(row == 0, 0.0, pltpu.roll(run, 1, 0))
    f1[0, 0] = prod[SUB - 1 : SUB, :]
    f1[0, 1] = run[SUB - 1 : SUB, :]

    pl.semaphore_wait(barrier, len(peers))
    fwd1 = to_group(0, f1)
    xcopies = to_batch(0, lambda d: xall.at[0], lambda d: xall.at[d])

    bp = jnp.ones((SUB, chans), f32)
    for j in range(steps - 1, -1, -1):
        bp = take(dec, j + 1) * bp
        bprod[j] = bp
    bshift = {}
    shift = 1
    while shift < SUB:
        seg[4 + len(bshift)] = bp
        bshift[shift] = 4 + len(bshift)
        bp = jnp.where(row < SUB - shift, bp * pltpu.roll(bp, SUB - shift, 0), bp)
        shift *= 2
    seg[2] = jnp.where(row == SUB - 1, 1.0, pltpu.roll(bp, SUB - 1, 0))

    one = jnp.ones((1, chans), f32)
    zero = jnp.zeros((1, chans), f32)
    arrive(fwd1)
    pre_p, pre_s, tot_p, tot_s = one, zero, one, zero
    for k in range(gs):
        slot = (mem - k + gs) % gs
        pk, sk = f1[slot, 0], f1[slot, 1]
        reached = k < mem
        pre_s = lax.select(reached, pk * pre_s + sk, pre_s)
        pre_p = lax.select(reached, pk * pre_p, pre_p)
        tot_s = pk * tot_s + sk
        tot_p = pk * tot_p
    f2[0, 0] = tot_p
    f2[0, 1] = tot_s
    fwd2 = to_line(0, f2)
    arrive(fwd2)
    far = zero
    for k in range(ng):
        slot = (grp - k + ng) % ng
        far = lax.select(k < grp, f2[slot, 0] * far + f2[slot, 1], far)
    entering = pre_p * far + pre_s

    carry = seg[1] + seg[0] * entering
    for j in range(steps):
        states = (part[j] + fprod[j] * carry).astype(bf16).astype(f32)
        put(sblk, j, states)
    scopies = to_batch(1, lambda d: sblk.at[in_batch[d]], lambda d: sall.at[d])
    sall[0] = sblk[mb]
    state_b = jnp.concatenate([sblk[l // nch, l % nch].astype(bf16) for l in range(lanes)], axis=1)
    mixed = lax.dot_general(state_b, out_ref[...], (((1,), (1,)), ((), ())), preferred_element_type=f32)
    outputs = (inputs_ref[...].astype(f32) + mixed).astype(bf16)
    outputs_ref[...] = outputs
    errors = (outputs.astype(f32) - target_ref[...].astype(f32)).astype(bf16)
    eall[0] = errors.astype(f32)
    ecopies = to_batch(2, lambda d: eall.at[0], lambda d: eall.at[d])
    spread(val, jnp.dot(errors, out_ref[...], preferred_element_type=f32))

    run = jnp.zeros((SUB, chans), f32)
    for j in range(steps - 1, -1, -1):
        run = take(dec, j + 1) * run + take(val, j)
        part[j] = run
    for shift, at in bshift.items():
        run = jnp.where(row < SUB - shift, seg[at] * pltpu.roll(run, SUB - shift, 0) + run, run)
    seg[3] = jnp.where(row == SUB - 1, 0.0, pltpu.roll(run, SUB - 1, 0))
    b1[0] = jnp.concatenate([dec[l, 0:1, :] for l in range(lanes)], axis=1) * run[0:1, :]
    bwd1 = to_group(1, b1)

    def term(which, lhs, rhs):
        lhs = lhs[...].reshape(nb * length, width).astype(bf16)
        for c in range(nch):
            block = lax.dot_general(
                lhs, rhs[:, c].reshape(nb * length, cw).astype(bf16),
                (((0,), (0,)), ((), ())), preferred_element_type=f32,
            )
            acc[which, c] = block.reshape((2,) * nbits + (rows, cw))

    def order(c):
        seq = list(range(nbits))
        if c % 2 and nbits > 1:
            seq[0], seq[1] = 1, 0
        return seq

    def place(seq, p, mine):
        at = [slice(None)] * nbits
        for q in seq[:p]:
            at[nbits - 1 - q] = bits[q]
        q = seq[p]
        at[nbits - 1 - q] = bits[q] if mine else 1 - bits[q]
        return tuple(at)

    flying = {}

    def halve_send(which, p):
        for c in range(nch):
            seq = order(c)
            q = seq[p]
            other = me + (1 - 2 * bits[q]) * (1 << q)
            flying[which, c] = send(
                acc.at[(which, c) + place(seq, p, False)], recvs[p].at[which, c],
                rss.at[which, c, p], rsr.at[which, c, p], (other, mb),
            )

    def halve_add(which, p):
        for c in range(nch):
            seq = order(c)
            flying[which, c].wait_recv()
            at = place(seq, p, True)
            free = [i for i in range(nbits) if isinstance(at[i], slice)]
            for n in range(1 << len(free)):
                digits = [(n >> (len(free) - 1 - i)) & 1 for i in range(len(free))]
                full = list(at)
                for i, v in zip(free, digits):
                    full[i] = v
                full = (which, c) + tuple(full)
                acc[full] = acc[full] + recvs[p][(which, c) + tuple(digits)]

    arrive(scopies)
    arrive(ecopies)
    term(0, eall, sall)
    halve_send(0, 0)

    arrive(bwd1)
    suf_p, suf_b, tot_b = one, zero, zero
    for k in range(gs - 1, -1, -1):
        slot = (mem - k + gs) % gs
        pk, bk = f1[slot, 0], b1[slot]
        reached = k > mem
        suf_b = lax.select(reached, pk * suf_b + bk, suf_b)
        suf_p = lax.select(reached, pk * suf_p, suf_p)
        tot_b = pk * tot_b + bk
    b2[0] = tot_b
    bwd2 = to_line(1, b2)
    arrive(bwd2)
    far = zero
    for k in range(ng - 1, -1, -1):
        slot = (grp - k + ng) % ng
        far = lax.select(k > grp, f2[slot, 0] * far + b2[slot], far)
    arriving = suf_p * far + suf_b

    carry = seg[3] + seg[2] * arriving
    for j in range(steps):
        grads = (take(gat, j) * (part[j] + bprod[j] * carry)).astype(bf16).astype(f32)
        put(dblk, j, grads)
    dcopies = to_batch(3, lambda d: dblk.at[in_batch[d]], lambda d: dall.at[d])
    dall[0] = dblk[mb]
    arrive(xcopies)
    arrive(dcopies)
    term(1, xall, dall)
    halve_send(1, 0)

    def finish(which):
        for c in range(nch):
            raw[which, mb, :, c * cw : (c + 1) * cw] = acc[(which, c) + tuple(bits[::-1])]
        return to_batch(4 + which, lambda d: raw.at[which, mb], lambda d: raw.at[which, mb])

    for p in range(nbits):
        halve_add(0, p)
        if p + 1 < nbits:
            halve_send(0, p + 1)
        else:
            ocopies = finish(0)
        halve_add(1, p)
        if p + 1 < nbits:
            halve_send(1, p + 1)
        else:
            icopies = finish(1)
    arrive(ocopies)
    arrive(icopies)

    squares = jnp.zeros((SUB, 128), f32)
    for which in range(2):
        for p in range(nb):
            block = raw[which, p]
            block = block * block
            for r in range(0, rows, SUB):
                for c in range(0, cols, 128):
                    squares = squares + block[r : r + SUB, c : c + 128]
    q1[0] = squares
    arrive(to_group(2, q1))
    total = q1[0]
    for d in range(1, gs):
        total = total + q1[d]
    q2[0] = total
    arrive(to_line(2, q2))
    total = q2[0]
    for d in range(1, ng):
        total = total + q2[d]
    total = jnp.sum(jnp.sum(total, axis=0, keepdims=True), axis=1, keepdims=True)
    rms = jnp.sqrt(total / (2.0 * width * chans) + 1e-06)
    factor = jnp.minimum(1.0, 1.0 / rms)
    for p in range(nb):
        gout_ref[:, p * cols : (p + 1) * cols] = factor * raw[0, p]
        gin_ref[:, p * cols : (p + 1) * cols] = factor * raw[1, p]
    for cp in pending:
        cp.wait_send()


def shards(nt, nb, inputs, rates, target, in_proj, out_proj):
    _, length, width = inputs.shape
    chans = in_proj.shape[1]
    nbits = nt.bit_length() - 1
    gs = 1 << (nbits // 2)
    ng = nt // gs
    rows, cols = width // nt, chans // nb
    nch, cw, lanes = cols // LANE, LANE, chans // LANE
    steps = length // SUB
    f32 = jnp.float32
    vmem, dma = pltpu.VMEM, pltpu.SemaphoreType.DMA
    scratch = [
        vmem((lanes, length + SUB, LANE), f32),
        vmem((lanes, length, LANE), f32),
        vmem((lanes, length, LANE), f32),
        vmem((steps, SUB, chans), f32),
        vmem((steps, SUB, chans), f32),
        vmem((steps, SUB, chans), f32),
        vmem((7, SUB, chans), f32),
        vmem((nb, length, width), f32),
        vmem((nb, length, width), f32),
        vmem((nb, nch, length, LANE), f32),
        vmem((nb, nch, length, LANE), f32),
        vmem((nb, nch, length, LANE), f32),
        vmem((nb, nch, length, LANE), f32),
        vmem((gs, 2, 1, chans), f32),
        vmem((ng, 2, 1, chans), f32),
        vmem((gs, 1, chans), f32),
        vmem((ng, 1, chans), f32),
        vmem((gs, SUB, 128), f32),
        vmem((ng, SUB, 128), f32),
        vmem((2, nb, rows, cols), f32),
        vmem((2, nch) + (2,) * nbits + (rows, cw), f32),
    ]
    scratch += [vmem((2, nch) + (2,) * (nbits - 1 - p) + (rows, cw), f32) for p in range(nbits)]
    scratch += [dma((3, gs))] * 2 + [dma((3, ng))] * 2 + [dma((6, nb))] * 2 + [dma((2, nch, nbits))] * 2
    spec = pl.BlockSpec(memory_space=pltpu.VMEM)
    outputs, grad_in, grad_out = pl.pallas_call(
        functools.partial(kernel, nt, nb),
        out_shape=(
            jax.ShapeDtypeStruct((length, width), jnp.bfloat16),
            jax.ShapeDtypeStruct((rows, chans), f32),
            jax.ShapeDtypeStruct((rows, chans), f32),
        ),
        in_specs=[spec] * 5,
        out_specs=(spec,) * 3,
        scratch_shapes=scratch,
        compiler_params=pltpu.CompilerParams(
            collective_id=0, has_side_effects=True, vmem_limit_bytes=60 * 1024 * 1024
        ),
    )(inputs[0], rates[0], target[0], in_proj, out_proj)
    return outputs[None], grad_in, grad_out


def solution(mesh):
    return jax.shard_map(
        functools.partial(shards, mesh.shape["tm"], mesh.shape["batch"]),
        mesh=mesh,
        in_specs=(P("batch", "tm", None), P("batch", "tm", None), P("batch", "tm", None), P(), P()),
        out_specs=(P("batch", "tm", None), P("tm", None), P("tm", None)),
        check_vma=False,
    )
```

```python
import functools

import jax
import jax.numpy as jnp
from jax import lax
from jax.experimental import pallas as pl
from jax.experimental.pallas import tpu as pltpu
from jax.sharding import PartitionSpec as P

MESH = pl.DeviceIdType.MESH
SUB = 8
LANE = 128
VMEM_LIMIT = 60 * 1024 * 1024


def gate_of(rates, decays):
    sq = rates * rates
    poly = 1.0 / 39916800.0
    for den in (362880.0, 5040.0, 120.0, 6.0):
        poly = poly * sq + 1.0 / den
    poly = poly * sq + 1.0
    return jnp.sqrt(2.0 * decays * rates * poly)


def kernel(
    nt, nb, inputs_hbm, rates_hbm, target_hbm, in_hbm, out_hbm,
    outputs_ref, raw_ref, total_ref,
    inputs_ref, rates_ref, target_ref, in_ref, out_ref, loads,
    dec, gat, val, part, fprod, bprod, seg, xall, eall, sall, dall, sblk, dblk,
    f1, f2, b1, b2, q1, q2, raw, acc, line, *rest,
):
    nbits = (nt.bit_length() - 1) // 2
    recvs = rest[:nbits]
    c1s, c1r, c2s, c2r, xs, xr, rss, rsr, lss, lsr, qs, qr, ws, wr = rest[nbits:]
    gs = 1 << nbits
    ng = nt // gs
    copies_in = [
        pltpu.make_async_copy(src, dst, loads.at[i])
        for i, (src, dst) in enumerate([
            (rates_hbm, rates_ref), (inputs_hbm, inputs_ref), (in_hbm, in_ref),
            (out_hbm, out_ref), (target_hbm, target_ref),
        ])
    ]
    for cp in copies_in:
        cp.start()
    length, width = inputs_ref.shape
    chans = in_ref.shape[1]
    cols = chans // nb
    steps = length // SUB
    nch, rows, cw = acc.shape[1], acc.shape[-2], acc.shape[-1]
    lanes = chans // LANE
    f32, bf16 = jnp.float32, jnp.bfloat16

    me = lax.axis_index("tm")
    mb = lax.axis_index("batch")
    grp, mem = me // gs, me % gs
    bits = [(me // (1 << q)) % 2 for q in range(nbits)]

    in_group = [grp * gs + (mem + d) % gs for d in range(gs)]
    in_line = [((grp + d) % ng) * gs + mem for d in range(ng)]
    in_batch = [(mb + d) % nb for d in range(nb)]

    barrier = pltpu.get_barrier_semaphore()
    near = [(d, e) for d in range(gs) for e in range(nb) if d or e]
    peers = [(in_group[d], in_batch[e]) for d, e in near] + [(t, mb) for t in in_line[1:]]
    for peer in peers:
        pl.semaphore_signal(barrier, inc=1, device_id=peer, device_id_type=MESH)

    pending = []

    def send(src, dst, ssem, rsem, peer):
        cp = pltpu.make_async_remote_copy(
            src_ref=src, dst_ref=dst, send_sem=ssem, recv_sem=rsem, device_id=peer, device_id_type=MESH
        )
        cp.start()
        pending.append(cp)
        return cp

    def to_group(kind, buf):
        return [
            send(buf.at[0], buf.at[d], c1s.at[kind, d], c1r.at[kind, d], (in_group[d], mb)) for d in range(1, gs)
        ]

    def to_line(kind, buf):
        return [
            send(buf.at[0], buf.at[d], c2s.at[kind, d], c2r.at[kind, d], (in_line[d], mb)) for d in range(1, ng)
        ]

    def to_batch(kind, src_of, dst_of):
        return [
            send(src_of(d), dst_of(d), xs.at[kind, d], xr.at[kind, d], (me, in_batch[d])) for d in range(1, nb)
        ]

    def arrive(copies):
        for cp in copies:
            cp.wait_recv()

    def spread(ref, value):
        for l in range(lanes):
            ref[l] = value[:, l * LANE : (l + 1) * LANE]

    def take(ref, j):
        return jnp.concatenate([ref[l, pl.ds(j, SUB, stride=steps), :] for l in range(lanes)], axis=1)

    def put(ref, j, value):
        for l in range(lanes):
            ref[l // nch, l % nch, pl.ds(j, SUB, stride=steps), :] = value[:, l * LANE : (l + 1) * LANE]

    copies_in[0].wait()
    rates = rates_ref[...].astype(f32)
    decays = jnp.exp(-rates)
    for l in range(lanes):
        dec[l, 0:length, :] = decays[:, l * LANE : (l + 1) * LANE]
        dec[l, length : length + SUB, :] = jnp.ones((SUB, LANE), f32)
    gates = gate_of(rates, decays)
    spread(gat, gates)
    copies_in[1].wait()
    xall[0] = inputs_ref[...].astype(f32)
    copies_in[2].wait()
    spread(val, gates * jnp.dot(inputs_ref[...], in_ref[...], preferred_element_type=f32))

    row = lax.broadcasted_iota(jnp.int32, (SUB, chans), 0)

    run = jnp.zeros((SUB, chans), f32)
    prod = jnp.ones((SUB, chans), f32)
    for j in range(steps):
        d = take(dec, j)
        run = d * run + take(val, j)
        prod = d * prod
        part[j] = run
        fprod[j] = prod
    shift = 1
    while shift < SUB:
        keep = row >= shift
        run = jnp.where(keep, prod * pltpu.roll(run, shift, 0) + run, run)
        prod = jnp.where(keep, prod * pltpu.roll(prod, shift, 0), prod)
        shift *= 2
    seg[0] = jnp.where(row == 0, 1.0, pltpu.roll(prod, 1, 0))
    seg[1] = jnp.where(row == 0, 0.0, pltpu.roll(run, 1, 0))
    f1[0, 0] = prod[SUB - 1 : SUB, :]
    f1[0, 1] = run[SUB - 1 : SUB, :]

    pl.semaphore_wait(barrier, len(peers))
    fwd1 = to_group(0, f1)
    xcopies = to_batch(0, lambda d: xall.at[0], lambda d: xall.at[d])

    copies_in[3].wait()
    copies_in[4].wait()

    bp = jnp.ones((SUB, chans), f32)
    for j in range(steps - 1, -1, -1):
        bp = take(dec, j + 1) * bp
        bprod[j] = bp
    bshift = {}
    shift = 1
    while shift < SUB:
        seg[4 + len(bshift)] = bp
        bshift[shift] = 4 + len(bshift)
        bp = jnp.where(row < SUB - shift, bp * pltpu.roll(bp, SUB - shift, 0), bp)
        shift *= 2
    seg[2] = jnp.where(row == SUB - 1, 1.0, pltpu.roll(bp, SUB - 1, 0))

    one = jnp.ones((1, chans), f32)
    zero = jnp.zeros((1, chans), f32)
    arrive(fwd1)
    pre_p, pre_s, tot_p, tot_s = one, zero, one, zero
    for k in range(gs):
        slot = (mem - k + gs) % gs
        pk, sk = f1[slot, 0], f1[slot, 1]
        reached = k < mem
        pre_s = lax.select(reached, pk * pre_s + sk, pre_s)
        pre_p = lax.select(reached, pk * pre_p, pre_p)
        tot_s = pk * tot_s + sk
        tot_p = pk * tot_p
    f2[0, 0] = tot_p
    f2[0, 1] = tot_s
    fwd2 = to_line(0, f2)
    arrive(fwd2)
    far = zero
    for k in range(ng):
        slot = (grp - k + ng) % ng
        far = lax.select(k < grp, f2[slot, 0] * far + f2[slot, 1], far)
    entering = pre_p * far + pre_s

    carry = seg[1] + seg[0] * entering
    for j in range(steps):
        states = (part[j] + fprod[j] * carry).astype(bf16).astype(f32)
        put(sblk, j, states)
    scopies = to_batch(1, lambda d: sblk.at[in_batch[d]], lambda d: sall.at[d])
    sall[0] = sblk[mb]
    state_b = jnp.concatenate([sblk[l // nch, l % nch].astype(bf16) for l in range(lanes)], axis=1)
    mixed = lax.dot_general(state_b, out_ref[...], (((1,), (1,)), ((), ())), preferred_element_type=f32)
    outputs = (inputs_ref[...].astype(f32) + mixed).astype(bf16)
    outputs_ref[...] = outputs
    errors = (outputs.astype(f32) - target_ref[...].astype(f32)).astype(bf16)
    eall[0] = errors.astype(f32)
    ecopies = to_batch(2, lambda d: eall.at[0], lambda d: eall.at[d])
    spread(val, jnp.dot(errors, out_ref[...], preferred_element_type=f32))

    run = jnp.zeros((SUB, chans), f32)
    for j in range(steps - 1, -1, -1):
        run = take(dec, j + 1) * run + take(val, j)
        part[j] = run
    for shift, at in bshift.items():
        run = jnp.where(row < SUB - shift, seg[at] * pltpu.roll(run, SUB - shift, 0) + run, run)
    seg[3] = jnp.where(row == SUB - 1, 0.0, pltpu.roll(run, SUB - 1, 0))
    b1[0] = jnp.concatenate([dec[l, 0:1, :] for l in range(lanes)], axis=1) * run[0:1, :]
    bwd1 = to_group(1, b1)

    def term(which, lhs, rhs):
        lhs = lhs[...].reshape(nb * length, width).astype(bf16)
        for wave in waves:
            for c in wave:
                block = lax.dot_general(
                    lhs, rhs[:, c].reshape(nb * length, cw).astype(bf16),
                    (((0,), (0,)), ((), ())), preferred_element_type=f32,
                )
                acc[which, c] = block.reshape((ng,) + (2,) * nbits + (rows, cw))
            halve_send(which, wave, 0)

    waves = [range(c, min(c + 2, nch)) for c in range(0, nch, 2)]

    def order(c):
        seq = list(range(nbits))
        if c % 2 and nbits > 1:
            seq[0], seq[1] = 1, 0
        return seq

    def place(seq, p, mine):
        at = [slice(None)] * nbits
        for q in seq[:p]:
            at[nbits - 1 - q] = bits[q]
        q = seq[p]
        at[nbits - 1 - q] = bits[q] if mine else 1 - bits[q]
        return tuple(at)

    flying = {}

    def halve_send(which, wave, p):
        for c in wave:
            seq = order(c)
            q = seq[p]
            other = me + (1 - 2 * bits[q]) * (1 << q)
            flying[which, c] = send(
                acc.at[(which, c, slice(None)) + place(seq, p, False)], recvs[p].at[which, c],
                rss.at[which, c, p], rsr.at[which, c, p], (other, mb),
            )

    def halve_add(which, wave, p):
        for c in wave:
            flying[which, c].wait_recv()
            at = place(order(c), p, True)
            free = [i for i in range(nbits) if isinstance(at[i], slice)]
            for n in range(1 << len(free)):
                digits = [(n >> (len(free) - 1 - i)) & 1 for i in range(len(free))]
                full = list(at)
                for i, v in zip(free, digits):
                    full[i] = v
                for g in range(ng):
                    here = (which, c, g) + tuple(full)
                    acc[here] = acc[here] + recvs[p][(which, c, g) + tuple(digits)]

    def step(which, wave, p):
        halve_add(which, wave, p)
        if p + 1 < nbits:
            halve_send(which, wave, p + 1)
        else:
            for c in wave:
                flying[which, c] = [
                    send(
                        acc.at[(which, c, (grp + d) % ng) + tuple(bits[::-1])], line.at[which, c, d],
                        lss.at[which, c, d], lsr.at[which, c, d], (in_line[d], mb),
                    )
                    for d in range(1, ng)
                ]

    raw_copies = []

    def finish(which, wave):
        for c in wave:
            arrive(flying[which, c])
            own = acc[(which, c, grp) + tuple(bits[::-1])]
            for d in range(1, ng):
                own = own + line[which, c, d]
            raw[which, mb, c] = own
            for d in range(1, nb):
                raw_copies.append(
                    send(
                        raw.at[which, mb, c], raw.at[which, mb, c], ws.at[which, c, d], wr.at[which, c, d],
                        (me, in_batch[d]),
                    )
                )

    arrive(scopies)
    arrive(ecopies)
    term(0, eall, sall)

    arrive(bwd1)
    suf_p, suf_b, tot_b = one, zero, zero
    for k in range(gs - 1, -1, -1):
        slot = (mem - k + gs) % gs
        pk, bk = f1[slot, 0], b1[slot]
        reached = k > mem
        suf_b = lax.select(reached, pk * suf_b + bk, suf_b)
        suf_p = lax.select(reached, pk * suf_p, suf_p)
        tot_b = pk * tot_b + bk
    b2[0] = tot_b
    bwd2 = to_line(1, b2)
    step(0, waves[0], 0)
    arrive(bwd2)
    far = zero
    for k in range(ng - 1, -1, -1):
        slot = (grp - k + ng) % ng
        far = lax.select(k > grp, f2[slot, 0] * far + b2[slot], far)
    arriving = suf_p * far + suf_b

    carry = seg[3] + seg[2] * arriving
    for j in range(steps):
        grads = (take(gat, j) * (part[j] + bprod[j] * carry)).astype(bf16).astype(f32)
        put(dblk, j, grads)
    dcopies = to_batch(3, lambda d: dblk.at[in_batch[d]], lambda d: dall.at[d])
    dall[0] = dblk[mb]
    arrive(xcopies)
    for wave in waves[1:]:
        step(0, wave, 0)
    arrive(dcopies)
    term(1, xall, dall)

    for p in range(1, nbits):
        for wave in waves:
            step(0, wave, p)
    step(1, waves[0], 0)
    for wave in waves:
        finish(0, wave)
    for wave in waves[1:]:
        step(1, wave, 0)
    for p in range(1, nbits):
        for wave in waves:
            step(1, wave, p)
    for wave in waves:
        finish(1, wave)

    squares = jnp.zeros((SUB, LANE), f32)
    for which in range(2):
        for c in range(nch):
            block = raw[which, mb, c]
            block = block * block
            for at in range(0, rows, SUB):
                squares = squares + block[at : at + SUB]
    q1[0, mb] = squares
    arrive([
        send(q1.at[0, mb], q1.at[d, mb], qs.at[d, e], qr.at[d, e], (in_group[d], in_batch[e])) for d, e in near
    ])
    total = jnp.zeros((SUB, LANE), f32)
    for d in range(gs):
        for e in range(nb):
            total = total + q1[d, e]
    q2[0] = total
    qcopies = to_line(2, q2)
    arrive(raw_copies)
    for which in range(2):
        for p in range(nb):
            for c in range(nch):
                at = p * cols + c * cw
                raw_ref[which, :, at : at + cw] = raw[which, p, c]
    arrive(qcopies)
    total = q2[0]
    for d in range(1, ng):
        total = total + q2[d]
    total_ref[...] = total
    for cp in pending:
        cp.wait_send()


def scaled(width, chans, outputs_in, raw_ref, total_ref, outputs_ref, gin_ref, gout_ref):
    total = jnp.sum(jnp.sum(total_ref[...], axis=0, keepdims=True), axis=1, keepdims=True)
    rms = jnp.sqrt(total / (2.0 * width * chans) + 1e-06)
    factor = jnp.minimum(1.0, 1.0 / rms)
    outputs_ref[...] = outputs_in[...]
    gout_ref[...] = factor * raw_ref[0]
    gin_ref[...] = factor * raw_ref[1]


def shards(nt, nb, inputs, rates, target, in_proj, out_proj):
    _, length, width = inputs.shape
    chans = in_proj.shape[1]
    nbits = (nt.bit_length() - 1) // 2
    gs = 1 << nbits
    ng = nt // gs
    rows, cols = width // nt, chans // nb
    nch, cw, lanes = cols // LANE, LANE, chans // LANE
    steps = length // SUB
    f32 = jnp.float32
    vmem, dma = pltpu.VMEM, pltpu.SemaphoreType.DMA
    scratch = [
        vmem((length, width), jnp.bfloat16),
        vmem((length, chans), jnp.bfloat16),
        vmem((length, width), jnp.bfloat16),
        vmem((width, chans), jnp.bfloat16),
        vmem((width, chans), jnp.bfloat16),
        dma((5,)),
        vmem((lanes, length + SUB, LANE), f32),
        vmem((lanes, length, LANE), f32),
        vmem((lanes, length, LANE), f32),
        vmem((steps, SUB, chans), f32),
        vmem((steps, SUB, chans), f32),
        vmem((steps, SUB, chans), f32),
        vmem((7, SUB, chans), f32),
        vmem((nb, length, width), f32),
        vmem((nb, length, width), f32),
        vmem((nb, nch, length, LANE), f32),
        vmem((nb, nch, length, LANE), f32),
        vmem((nb, nch, length, LANE), f32),
        vmem((nb, nch, length, LANE), f32),
        vmem((gs, 2, 1, chans), f32),
        vmem((ng, 2, 1, chans), f32),
        vmem((gs, 1, chans), f32),
        vmem((ng, 1, chans), f32),
        vmem((gs, nb, SUB, LANE), f32),
        vmem((ng, SUB, LANE), f32),
        vmem((2, nb, nch, rows, cw), f32),
        vmem((2, nch, ng) + (2,) * nbits + (rows, cw), f32),
        vmem((2, nch, ng, rows, cw), f32),
    ]
    scratch += [vmem((2, nch, ng) + (2,) * (nbits - 1 - p) + (rows, cw), f32) for p in range(nbits)]
    scratch += [dma((2, gs))] * 2 + [dma((3, ng))] * 2 + [dma((4, nb))] * 2 + [dma((2, nch, nbits))] * 2
    scratch += [dma((2, nch, ng))] * 2 + [dma((gs, nb))] * 2 + [dma((2, nch, nb))] * 2
    spec = pl.BlockSpec(memory_space=pltpu.VMEM)
    held = (
        jax.ShapeDtypeStruct((length, width), jnp.bfloat16),
        jax.ShapeDtypeStruct((2, rows, chans), f32),
        jax.ShapeDtypeStruct((SUB, LANE), f32),
    )
    parts = pl.pallas_call(
        functools.partial(kernel, nt, nb),
        out_shape=held,
        in_specs=[pl.BlockSpec(memory_space=pl.ANY)] * 5,
        out_specs=(spec,) * 3,
        scratch_shapes=scratch,
        compiler_params=pltpu.CompilerParams(
            collective_id=0, has_side_effects=True, vmem_limit_bytes=VMEM_LIMIT
        ),
    )(inputs[0], rates[0], target[0], in_proj, out_proj)
    outputs, grad_in, grad_out = pl.pallas_call(
        functools.partial(scaled, width, chans),
        out_shape=(
            held[0],
            jax.ShapeDtypeStruct((rows, chans), f32),
            jax.ShapeDtypeStruct((rows, chans), f32),
        ),
        in_specs=[spec] * 3,
        out_specs=(spec,) * 3,
    )(*parts)
    return outputs[None], grad_in, grad_out


def solution(mesh):
    return jax.shard_map(
        functools.partial(shards, mesh.shape["tm"], mesh.shape["batch"]),
        mesh=mesh,
        in_specs=(P("batch", "tm", None), P("batch", "tm", None), P("batch", "tm", None), P(), P()),
        out_specs=(P("batch", "tm", None), P("tm", None), P("tm", None)),
        check_vma=False,
    )
```
